32 devices in a mesh: row: 4 (over y, x), col: 4 (over z), layer: 2 (over core).
Axes of the slice: x: 2, y: 2, z: 4, core: 2. Of those that a mesh axis runs over, the one named last changes fastest.
Arguments:
- blocks: float32 [4, 4, 2, 8, 128, 128], P('row', 'col', 'layer'), may hold values from -0.5 to 0.5
- block_ids: int32 [4, 4, 2, 8], P('row', 'col', 'layer'), may hold values from 0 to 143, as said below
- counts: int32 [4, 4, 2], P('row', 'col', 'layer'), may hold values from 0 to 8, as said below
Outputs:
- purified: float32 [6144, 6144], P(('row', 'layer'), 'col')
The draws below stay inside these ranges and needn't reach their ends.
Inputs may be any that keep to these rules, and one draw needn't show every extreme that they name: `block_ids`: within one tile the 2 x 8 slots named over all layers are distinct. `counts`: A tile's live blocks fill the list of layer 0 before that of the next layer; some device's list is full in every draw.
All inputs are finite; a program needn't handle non-finite values.
Results may differ from the reference program's by a relative error of at most 0.000075.
Values sent between devices are 32-bit elements; how exact they have to be, the bound alone decides.
No kernel may reach another device: no remote copies, remote signals or barrier semaphores. Data moves between devices by JAX's collectives and lax.ppermute only.
A program may use at most 320 MiB of HBM per device.

```python
import jax
import jax.numpy as jnp
from jax import lax

BLOCK = 128
ROW_BLOCKS = 12
LIST = 8
COL_BLOCKS = 12
N_ROW = 4
N_COL = 4
N_LAYER = 2


def draw_block_ids(key, part):
    tiles = N_ROW * N_COL
    slots = ROW_BLOCKS * COL_BLOCKS
    noise = jax.random.randint(jax.random.fold_in(key, 11), (tiles, slots), 0, 2 ** 16)
    scores = noise * slots + jnp.arange(slots, dtype=jnp.int32)[None, :]
    order = jnp.argsort(scores, axis=1).astype(jnp.int32)
    return order[:, :N_LAYER * LIST].reshape(N_ROW, N_COL, N_LAYER, LIST)


def draw_counts(key, part):
    tiles = N_ROW * N_COL
    capacity = N_LAYER * LIST
    keep = jax.random.randint(jax.random.fold_in(key, 23), (tiles,), max(capacity // 2, 1), capacity + 1)
    fullest = jax.random.randint(jax.random.fold_in(key, 29), (), 0, tiles).astype(jnp.int32)
    keep = jnp.where(jnp.arange(tiles, dtype=jnp.int32) == fullest, capacity, keep)
    layer_start = jnp.arange(N_LAYER, dtype=jnp.int32)[None, :] * LIST
    per_layer = jnp.clip(keep[:, None] - layer_start, 0, LIST)
    return per_layer.reshape(N_ROW, N_COL, N_LAYER).astype(jnp.int32)


def steps_of(rng, extent, shards, smallest, largest):
    loudness = 1.0
    for dim, blocks in shards:
        steps = jax.random.uniform(jax.random.fold_in(jax.random.fold_in(rng, 6), dim), (blocks,), jnp.float32, smallest / len(shards), largest / len(shards))
        loudness = loudness * jnp.repeat(jnp.exp(steps), extent[dim] // blocks).reshape((-1,) + (1,) * (len(extent) - 1 - dim))
    return loudness


def bell_draw(own_key, extent, deviation, bound, pieces=(), held_as=jnp.bfloat16):
    array = deviation * jax.random.normal(own_key, extent, jnp.float32)
    if pieces:
        array = array * steps_of(own_key, extent, pieces, -0.22, 0.18)
    return jnp.clip(array, -bound, bound).astype(held_as)


def setup_inputs(seed: int = 0) -> dict:
    seeds = jax.random.split(jax.random.key(seed), 4)
    return {
        "blocks": bell_draw(seeds[0], (N_ROW, N_COL, N_LAYER, LIST, BLOCK, BLOCK), 0.08, 0.5, ((0, 4), (1, 4), (2, 2)), jnp.float32),
        "block_ids": draw_block_ids(jax.random.fold_in(seeds[3], 71), 0),
        "counts": draw_counts(jax.random.fold_in(seeds[3], 71), 0),
    }


def reference(blocks, block_ids, counts):
    nblk = ROW_BLOCKS * N_ROW
    cblk = nblk // N_COL
    shape = (N_ROW, N_COL, N_LAYER, LIST)
    tile_row = lax.broadcasted_iota(jnp.int32, shape, 0)
    tile_col = lax.broadcasted_iota(jnp.int32, shape, 1)
    position = lax.broadcasted_iota(jnp.int32, shape, 3)
    glob_row = tile_row * ROW_BLOCKS + block_ids // cblk
    glob_col = tile_col * cblk + block_ids % cblk
    alive = position < counts[..., None]
    values = jnp.where(alive[..., None, None], blocks, jnp.float32(0.0))
    dense = jnp.zeros((nblk, BLOCK, nblk, BLOCK), jnp.float32)
    dense = dense.at[glob_row.reshape(-1), :, glob_col.reshape(-1), :].add(values.reshape(-1, BLOCK, BLOCK))
    matrix = dense.reshape(nblk * BLOCK, nblk * BLOCK)
    square = jnp.dot(matrix, matrix, precision=lax.Precision.HIGHEST, preferred_element_type=jnp.float32)
    cubed = jnp.dot(square, matrix, precision=lax.Precision.HIGHEST, preferred_element_type=jnp.float32)
    return 3.0 * square - 2.0 * cubed
```

```python
import functools

import jax
import jax.numpy as jnp
from jax import lax
from jax.experimental import pallas as pl
from jax.experimental.pallas import tpu as pltpu
from jax.sharding import PartitionSpec as P

ROW_BLOCKS = 12
DEPTH = 4
GROUP = 4
AXES = ("row", "col", "layer")


def split(x):
    high = x.astype(jnp.bfloat16)
    low = (x - high.astype(jnp.float32)).astype(jnp.bfloat16)
    return high, low


def kernel(
    sizes,
    where_ref,
    meta_ref,
    blocks_ref,
    out_ref,
    buffer,
    sem,
    left,
    right,
    panel,
    square,
    wide,
    head,
    nxt,
    left_row,
    chead,
    cnext,
    ccol,
    plan,
):
    n_row, n_col, n_layer, listed, side = sizes
    nblk = ROW_BLOCKS * n_row
    cblk = nblk // n_col
    half = ROW_BLOCKS // n_layer
    rows = half * side
    per_row = n_col * n_layer
    chunks = n_row * per_row
    my_row, my_col, my_layer = where_ref[0], where_ref[1], where_ref[2]

    def fetch(chunk, slot):
        return pltpu.make_async_copy(
            blocks_ref.at[pl.ds(chunk * listed, listed)], buffer.at[slot], sem.at[slot]
        )

    def clear(i, _):
        head[i] = -1
        chead[i] = -1
        return 0

    lax.fori_loop(0, nblk, clear, 0)
    base = my_row * per_row
    for d in range(DEPTH):
        fetch(base + d, d).start()

    def load_left(t, count):
        slot = lax.rem(t, DEPTH)
        chunk = base + t
        fetch(chunk, slot).wait()
        col = t // n_layer

        def one(s, count):
            ident = meta_ref[chunk, s]
            row = ident // cblk - my_layer * half
            use = (s < meta_ref[chunk, listed]) & (row >= 0) & (row < half)

            @pl.when(use)
            def _():
                k = col * cblk + lax.rem(ident, cblk)
                nxt[count] = head[k]
                head[k] = count
                left_row[count] = row
                high, low = split(buffer[slot, s])
                left[count, :, :side] = high
                left[count, :, side:] = low

            return count + use.astype(jnp.int32)

        count = lax.fori_loop(0, listed, one, count)

        @pl.when(t + DEPTH < per_row)
        def _():
            fetch(chunk + DEPTH, slot).start()

        return count

    lax.fori_loop(0, per_row, load_left, 0)

    for d in range(DEPTH):
        fetch(d, d).start()

    def zero(j, _):
        square[j] = jnp.zeros((rows, side), jnp.float32)
        return 0

    lax.fori_loop(0, nblk, zero, 0)
    for s in range(listed):
        right[s, side:, side:] = jnp.zeros((side, side), jnp.bfloat16)

    def stream(t, ccount):
        slot = lax.rem(t, DEPTH)
        row0 = t // per_row * ROW_BLOCKS
        col = lax.rem(t, per_row) // n_layer
        live = meta_ref[t, listed]
        fetch(t, slot).wait()

        def one(s, carry):
            count, ccount = carry
            ident = meta_ref[t, s]
            k = row0 + ident // cblk
            local = lax.rem(ident, cblk)
            alive = s < live
            mine = alive & (col == my_col)

            @pl.when(alive & ((head[k] >= 0) | mine))
            def _():
                high, low = split(buffer[slot, s])
                right[s, :side, :side] = high
                right[s, side:, :side] = high
                right[s, :side, side:] = low

            @pl.when(mine)
            def _():
                panel[ccount] = right[s]
                cnext[ccount] = chead[k]
                chead[k] = ccount
                ccol[ccount] = local

            def more(carry):
                return carry[0] >= 0

            def add(carry):
                a, count = carry
                plan[0, count] = a
                plan[1, count] = s
                plan[2, count] = col * cblk + local
                plan[3, count] = left_row[a]
                return nxt[a], count + 1

            first = jnp.where(alive, head[k], -1)
            _, count = lax.while_loop(more, add, (first, count))
            return count, ccount + mine.astype(jnp.int32)

        count, ccount = lax.fori_loop(0, listed, one, (0, ccount))

        @pl.when(t + DEPTH < chunks)
        def _():
            fetch(t + DEPTH, slot).start()

        for u in range(GROUP - 1):
            plan[0, count + u] = 0
            plan[1, count + u] = 0
            plan[2, count + u] = nblk
            plan[3, count + u] = 0

        def group(g, _):
            parts = []
            for u in range(GROUP):
                e = g * GROUP + u
                parts.append(
                    jnp.dot(
                        left[plan[0, e]], right[plan[1, e]], preferred_element_type=jnp.float32
                    )
                )
            for u in range(GROUP):
                e = g * GROUP + u
                at = pl.ds(pl.multiple_of(plan[3, e] * side, side), side)
                j = plan[2, e]
                square[j, at, :] = square[j, at, :] + (parts[u][:, :side] + parts[u][:, side:])
            return 0

        lax.fori_loop(0, (count + GROUP - 1) // GROUP, group, 0)
        return ccount

    lax.fori_loop(0, chunks, stream, 0)

    def first(j, _):
        at = pl.ds(pl.multiple_of(j * side, side), side)
        out_ref[:, at] = 3.0 * square[my_col * cblk + j]
        return 0

    lax.fori_loop(0, cblk, first, 0)

    def cube(k, _):
        @pl.when(chead[k] >= 0)
        def _():
            high, low = split(-2.0 * square[k])
            wide[:, :side] = high
            wide[:, side:] = low

            def more(c):
                return c >= 0

            def add(c):
                at = pl.ds(pl.multiple_of(ccol[c] * side, side), side)
                part = jnp.dot(wide[...], panel[c], preferred_element_type=jnp.float32)
                out_ref[:, at] = out_ref[:, at] + (part[:, :side] + part[:, side:])
                return cnext[c]

            lax.while_loop(more, add, chead[k])

        return 0

    lax.fori_loop(0, nblk, cube, 0)


def purify(sizes, where, meta, blocks):
    n_row, n_col, n_layer, listed, side = sizes
    nblk = ROW_BLOCKS * n_row
    cblk = nblk // n_col
    half = ROW_BLOCKS // n_layer
    rows = half * side
    lefts = min(n_col * n_layer * listed, half * nblk)
    mids = n_row * n_layer * listed
    return pl.pallas_call(
        functools.partial(kernel, sizes),
        out_shape=jax.ShapeDtypeStruct((rows, cblk * side), jnp.float32),
        in_specs=[
            pl.BlockSpec(memory_space=pltpu.SMEM),
            pl.BlockSpec(memory_space=pltpu.SMEM),
            pl.BlockSpec(memory_space=pl.ANY),
        ],
        out_specs=pl.BlockSpec(memory_space=pltpu.VMEM),
        scratch_shapes=[
            pltpu.VMEM((DEPTH, listed, side, side), jnp.float32),
            pltpu.SemaphoreType.DMA((DEPTH,)),
            pltpu.VMEM((lefts, side, 2 * side), jnp.bfloat16),
            pltpu.VMEM((listed, 2 * side, 2 * side), jnp.bfloat16),
            pltpu.VMEM((mids, 2 * side, 2 * side), jnp.bfloat16),
            pltpu.VMEM((nblk + 1, rows, side), jnp.float32),
            pltpu.VMEM((rows, 2 * side), jnp.bfloat16),
            pltpu.SMEM((nblk,), jnp.int32),
            pltpu.SMEM((lefts,), jnp.int32),
            pltpu.SMEM((lefts,), jnp.int32),
            pltpu.SMEM((nblk,), jnp.int32),
            pltpu.SMEM((mids,), jnp.int32),
            pltpu.SMEM((mids,), jnp.int32),
            pltpu.SMEM((4, listed * half + GROUP), jnp.int32),
        ],
        compiler_params=pltpu.CompilerParams(vmem_limit_bytes=62 * 1024 * 1024),
    )(where, meta, blocks)


def shards(blocks, block_ids, counts):
    n_row, n_col, n_layer = (lax.axis_size(a) for a in AXES)
    listed, side = blocks.shape[3], blocks.shape[-1]
    own = jnp.concatenate([block_ids.reshape(1, listed), counts.reshape(1, 1)], axis=1)
    meta = lax.all_gather(own, AXES, axis=0, tiled=True)
    values = lax.all_gather(blocks.reshape(listed, side, side), AXES, axis=0, tiled=True)
    where = jnp.stack([lax.axis_index(a) for a in AXES]).astype(jnp.int32)
    return purify((n_row, n_col, n_layer, listed, side), where, meta, values)


def solution(mesh):
    return jax.shard_map(
        shards,
        mesh=mesh,
        in_specs=(
            P("row", "col", "layer", None, None, None),
            P("row", "col", "layer", None),
            P("row", "col", "layer"),
        ),
        out_specs=P(("row", "layer"), "col"),
        check_vma=False,
    )
```

```python
import functools

import jax
import jax.numpy as jnp
from jax import lax
from jax.experimental import pallas as pl
from jax.experimental.pallas import tpu as pltpu
from jax.sharding import PartitionSpec as P

ROW_BLOCKS = 12
GROUP = 4
CHUNK = 768
PANEL_MB = 16
TILE_MB = 40
AXES = ("row", "col", "layer")
VMEM = pl.BlockSpec(memory_space=pltpu.VMEM)
SMEM = pl.BlockSpec(memory_space=pltpu.SMEM)
HBM = pl.BlockSpec(memory_space=pltpu.HBM)


def params(megabytes):
    return pltpu.CompilerParams(vmem_limit_bytes=megabytes * 1024 * 1024)


def split(x):
    high = x.astype(jnp.bfloat16)
    low = (x - high.astype(jnp.float32)).astype(jnp.bfloat16)
    return high, low


def product(left, right):
    part = jnp.dot(
        left, jnp.concatenate([right, right], axis=0), preferred_element_type=jnp.float32
    )
    side = right.shape[0]
    return part[:, :side] + part[:, side:]


def lanes(i, side):
    return pl.ds(pl.multiple_of(i * side, side), side)


def start_copies(side, listed, array_refs, buffer, lists, sem):
    out = []
    for i, ref in enumerate(array_refs):
        value = pltpu.make_async_copy(
            ref.at[pl.ds(0, listed * side)],
            buffer.at[pl.ds(i * listed * side, listed * side)],
            sem.at[0, i],
        )
        names = pltpu.make_async_copy(
            ref.at[pl.ds(listed * side, 8)], lists.at[pl.ds(i * 8, 8)], sem.at[1, i]
        )
        value.start()
        names.start()
        out.append((value, names))
    return out


def tile_row(segment, my_row, my_layer, n_layer):
    first, second, _, other = segment
    layer = (n_layer - 1 - my_layer) if other else my_layer
    return my_row ^ jnp.where(layer == 0, first, second)


def panel_kernel(sizes, kind, segments, where_ref, *refs):
    n_row, n_col, n_layer, listed, side = sizes
    arrays = len(segments)
    array_refs = refs[:arrays]
    panel, head, nxt, tag, buffer, lists, sem = refs[arrays:]
    nblk = ROW_BLOCKS * n_row
    cblk = nblk // n_col
    half = ROW_BLOCKS // n_layer
    my_row, my_col, my_layer = where_ref[0], where_ref[1], where_ref[2]
    moves = start_copies(side, listed, array_refs, buffer, lists, sem)

    def clear(i, _):
        head[i] = -1
        return 0

    lax.fori_loop(0, nblk, clear, 0)
    count = jnp.int32(0)
    for i, (value, names) in enumerate(moves):
        value.wait()
        names.wait()
        row = tile_row(segments[i], my_row, my_layer, n_layer)
        col = lax.rem(my_col + (n_col - segments[i][2]), n_col)
        live = lists[i * 8, listed].astype(jnp.int32)

        def one(s, count, i=i, row=row, col=col, live=live):
            ident = lists[i * 8, s].astype(jnp.int32)
            line = ident // cblk
            local = lax.rem(ident, cblk)
            if kind == "left":
                key, mark = col * cblk + local, line - my_layer * half
                use = (s < live) & (mark >= 0) & (mark < half)
            else:
                key, mark = row * ROW_BLOCKS + line, local
                use = s < live

            @pl.when(use)
            def _():
                nxt[count] = head[key]
                head[key] = count
                tag[count] = mark
                high, low = split(buffer[lanes(i * listed + s, side), :])
                panel[count, :, :side] = high
                panel[count, :, side:] = low

            return count + use.astype(jnp.int32)

        count = lax.fori_loop(0, listed, one, count)


def panel_call(sizes, kind, segments, arrays, most, where):
    n_row, n_col, n_layer, listed, side = sizes
    nblk = ROW_BLOCKS * n_row
    total = len(segments) * listed
    return pl.pallas_call(
        functools.partial(panel_kernel, sizes, kind, segments),
        out_shape=[
            jax.ShapeDtypeStruct((most, side, 2 * side), jnp.bfloat16),
            jax.ShapeDtypeStruct((nblk,), jnp.int32),
            jax.ShapeDtypeStruct((most,), jnp.int32),
            jax.ShapeDtypeStruct((most,), jnp.int32),
        ],
        in_specs=[SMEM] + [HBM] * len(arrays),
        out_specs=[VMEM, SMEM, SMEM, SMEM],
        scratch_shapes=[
            pltpu.VMEM((total * side, side), jnp.float32),
            pltpu.SMEM((len(segments) * 8, side), jnp.float32),
            pltpu.SemaphoreType.DMA((2, len(segments))),
        ],
        compiler_params=params(PANEL_MB),
        name=kind + "_panel",
    )(where, *arrays)


def tile_kernel(sizes, shifts, segments, *refs):
    n_row, n_col, n_layer, listed, side = sizes
    arrays = len(segments)
    where_ref, head, nxt, left_row, chead, cnext, ccol, left_ref, panel_ref = refs[:9]
    array_refs = refs[9 : 9 + arrays]
    rest = refs[9 + arrays :]
    if shifts[0]:
        before, rest = rest[0], rest[1:]
    out_ref, buffer, lists, sem, left, panel, late, right, square, wide, plan = rest
    nblk = ROW_BLOCKS * n_row
    cblk = nblk // n_col
    rows = ROW_BLOCKS // n_layer * side
    my_row, my_col, my_layer = where_ref[0], where_ref[1], where_ref[2]
    moves = start_copies(side, listed, array_refs, buffer, lists, sem)
    get_left = pltpu.make_async_copy(left_ref, left, late.at[0])
    get_panel = pltpu.make_async_copy(panel_ref, panel, late.at[1])
    get_left.start()
    get_panel.start()
    if shifts[0]:
        get_before = pltpu.make_async_copy(before, out_ref, late.at[2])
        get_before.start()
    for tile_shift in shifts:
        col = lax.rem(my_col + (n_col - tile_shift), n_col)

        def zero(j, _):
            square[j] = jnp.zeros((rows, side), jnp.float32)
            return 0

        lax.fori_loop(0, cblk, zero, 0)
        count = jnp.int32(0)
        for i, (value, names) in enumerate(moves):
            if segments[i][2] != tile_shift:
                continue
            value.wait()
            names.wait()
            row = tile_row(segments[i], my_row, my_layer, n_layer)
            live = lists[i * 8, listed].astype(jnp.int32)

            def one(s, count, i=i, row=row, live=live):
                ident = lists[i * 8, s].astype(jnp.int32)
                at = i * listed + s
                k = row * ROW_BLOCKS + ident // cblk
                local = lax.rem(ident, cblk)
                first = jnp.where(s < live, head[k], -1)

                @pl.when(first >= 0)
                def _():
                    high, low = split(buffer[lanes(at, side), :])
                    right[at, :, :side] = high
                    right[at, :, side:] = low

                def more(carry):
                    return carry[0] >= 0

                def add(carry):
                    a, count = carry
                    plan[0, count] = a
                    plan[1, count] = at
                    plan[2, count] = local
                    plan[3, count] = left_row[a]
                    return nxt[a], count + 1

                return lax.while_loop(more, add, (first, count))[1]

            count = lax.fori_loop(0, listed, one, count)

        for u in range(GROUP - 1):
            plan[0, count + u] = 0
            plan[1, count + u] = 0
            plan[2, count + u] = cblk
            plan[3, count + u] = 0

        def group(g, _):
            parts = []
            for u in range(GROUP):
                e = g * GROUP + u
                parts.append(product(left[plan[0, e]], right[plan[1, e]]))
            for u in range(GROUP):
                e = g * GROUP + u
                at = lanes(plan[3, e], side)
                j = plan[2, e]
                square[j, at, :] = square[j, at, :] + parts[u]
            return 0

        if tile_shift == shifts[0]:
            get_left.wait()
        lax.fori_loop(0, (count + GROUP - 1) // GROUP, group, 0)
        if tile_shift == shifts[0]:
            get_panel.wait()
            if tile_shift:
                get_before.wait()
        if not tile_shift:

            def begin(j, _):
                out_ref[:, lanes(j, side)] = 3.0 * square[j]
                return 0

            lax.fori_loop(0, cblk, begin, 0)

        def cube(j, _, col=col):
            k = col * cblk + j

            @pl.when(chead[k] >= 0)
            def _():
                high, low = split(-2.0 * square[j])
                wide[:, :side] = high
                wide[:, side:] = low

                def more(c):
                    return c >= 0

                def add(c):
                    at = lanes(ccol[c], side)
                    for m in range(0, rows, CHUNK):
                        line = pl.ds(m, CHUNK)
                        out_ref[line, at] = out_ref[line, at] + product(wide[line, :], panel[c])
                    return cnext[c]

                lax.while_loop(more, add, chead[k])

            return 0

        lax.fori_loop(0, cblk, cube, 0)


def tile_call(sizes, shifts, segments, arrays, where, lefts, rights, before):
    n_row, n_col, n_layer, listed, side = sizes
    nblk = ROW_BLOCKS * n_row
    cblk = nblk // n_col
    half = ROW_BLOCKS // n_layer
    rows = half * side
    total = len(segments) * listed
    left, head, nxt, left_row = lefts
    panel, chead, cnext, ccol = rights
    extra = [] if before is None else [before]
    return pl.pallas_call(
        functools.partial(tile_kernel, sizes, shifts, segments),
        out_shape=jax.ShapeDtypeStruct((rows, cblk * side), jnp.float32),
        in_specs=[SMEM] * 7 + [HBM] * (2 + len(arrays) + len(extra)),
        out_specs=VMEM,
        scratch_shapes=[
            pltpu.VMEM((total * side, side), jnp.float32),
            pltpu.SMEM((len(segments) * 8, side), jnp.float32),
            pltpu.SemaphoreType.DMA((2, len(segments))),
            pltpu.VMEM(left.shape, left.dtype),
            pltpu.VMEM(panel.shape, panel.dtype),
            pltpu.SemaphoreType.DMA((3,)),
            pltpu.VMEM((total, side, 2 * side), jnp.bfloat16),
            pltpu.VMEM((cblk + 1, rows, side), jnp.float32),
            pltpu.VMEM((rows, 2 * side), jnp.bfloat16),
            pltpu.SMEM((4, total * half + GROUP), jnp.int32),
        ],
        compiler_params=params(TILE_MB),
        name="tiles_" + "_".join(str(s) for s in shifts),
    )(where, head, nxt, left_row, chead, cnext, ccol, left, panel, *arrays, *extra)


def shards(blocks, block_ids, counts):
    n_row, n_col, n_layer = (lax.axis_size(a) for a in AXES)
    listed, side = blocks.shape[3], blocks.shape[-1]
    sizes = (n_row, n_col, n_layer, listed, side)
    half = ROW_BLOCKS // n_layer

    def flip(bits):
        pairs = []
        for r in range(n_row):
            for k in range(n_layer):
                pairs.append((r * n_layer + k, (r ^ bits[min(k, 1)]) * n_layer + k))
        return lambda y: lax.ppermute(y, ("row", "layer"), pairs)

    across, along = flip((1, 2)), flip((2, 1))

    def ring(y):
        return lax.ppermute(y, "col", [(i, (i + 1) % n_col) for i in range(n_col)])

    def sibling(y):
        return lax.ppermute(y, "layer", [(i, n_layer - 1 - i) for i in range(n_layer)])

    where = jnp.stack([lax.axis_index(a) for a in AXES]).astype(jnp.int32)
    names = jnp.concatenate([block_ids.reshape(listed), counts.reshape(1)]).astype(jnp.float32)
    names = jnp.pad(names.reshape(1, listed + 1), ((0, 7), (0, side - listed - 1)))
    own = jnp.concatenate([blocks.reshape(listed * side, side), names], axis=0)

    ways = {"A": (0, 0), "U": (1, 2), "V": (2, 1), "D": (3, 3)}
    held = {("A", 0): own}
    twin = {}
    lefts = rights = total = None
    fresh = [("A", 0)]

    def gathered(names):
        segments = [(*ways[k], s, other) for other in (False, True) for k, s in names]
        return segments, [source[name] for source in (held, twin) for name in names]

    def quads(shifts):
        return [(k, s) for s in shifts for k in ways]

    def tiles(shifts, total):
        for i in range(0, len(shifts), 2):
            segments, arrays = gathered(quads(shifts[i : i + 2]))
            total = tile_call(
                sizes, shifts[i : i + 2], segments, arrays, where, lefts, rights, total
            )
        return total

    for t in range(n_col + 2):
        sent = {}
        if t < n_col:
            sent[("U", t)] = across(held[("A", t)])
            sent[("V", t)] = along(held[("A", t)])
        if t < n_col - 1:
            sent[("A", t + 1)] = ring(held[("A", t)])
        if 1 <= t <= n_col:
            sent[("D", t - 1)] = along(held[("U", t - 1)])
        copied = {name: sibling(held[name]) for name in fresh}
        twin.update(copied)
        if t == 2:
            segments, arrays = gathered(quads([0]))
            most = n_row * n_layer * listed
            rights = panel_call(sizes, "right", segments, arrays, most, where)
        if t == n_col - 1:
            segments, arrays = gathered([("A", s) for s in range(n_col)])
            most = min(n_col * n_layer * listed, half * ROW_BLOCKS * n_row)
            lefts = panel_call(sizes, "left", segments, arrays, most, where)
            total = tiles(list(range(n_col - 3)), total)
        if t == n_col:
            total = tiles(list(range(n_col - 3, n_col - 1)), total)
        if t == n_col + 1:
            return tiles([n_col - 1], total)
        kept = lax.optimization_barrier((sent, copied, rights, lefts, total))
        sent, copied, rights, lefts, total = kept
        held.update(sent)
        twin.update(copied)
        fresh = list(sent)


def solution(mesh):
    return jax.shard_map(
        shards,
        mesh=mesh,
        in_specs=(
            P("row", "col", "layer", None, None, None),
            P("row", "col", "layer", None),
            P("row", "col", "layer"),
        ),
        out_specs=P(("row", "layer"), "col"),
        check_vma=False,
    )
```

```python
import functools

import jax
import jax.numpy as jnp
from jax import lax
from jax.experimental import pallas as pl
from jax.experimental.pallas import tpu as pltpu
from jax.sharding import PartitionSpec as P

ROW_BLOCKS = 12
GROUP = 4
AHEAD = (0, 1, 2, 3)
LATER = (0, 1, 1, 1)
CUBES = 8
CHUNK = 128
STRIP = 384
PANEL_MB = 61
TILE_MB = 61
AXES = ("row", "col", "layer")
VMEM = pl.BlockSpec(memory_space=pltpu.VMEM)
SMEM = pl.BlockSpec(memory_space=pltpu.SMEM)
HBM = pl.BlockSpec(memory_space=pltpu.HBM)


def params(megabytes):
    return pltpu.CompilerParams(vmem_limit_bytes=megabytes * 1024 * 1024)


def split(x):
    high = x.astype(jnp.bfloat16)
    low = (x - high.astype(jnp.float32)).astype(jnp.bfloat16)
    return high, low


def product(left, right):
    part = jnp.dot(
        left, jnp.concatenate([right, right], axis=0), preferred_element_type=jnp.float32
    )
    side = right.shape[0]
    return part[:, :side] + part[:, side:]


def lanes(i, side):
    return pl.ds(pl.multiple_of(i * side, side), side)


def start_copies(side, listed, array_refs, buffer, lists, sem):
    out = []
    for i, ref in enumerate(array_refs):
        value = pltpu.make_async_copy(
            ref.at[pl.ds(0, listed * side)],
            buffer.at[pl.ds(i * listed * side, listed * side)],
            sem.at[0, i],
        )
        names = pltpu.make_async_copy(
            ref.at[pl.ds(listed * side, 1)], lists.at[pl.ds(i, 1)], sem.at[1, i]
        )
        value.start()
        names.start()
        out.append((value, names))
    return out


def tile_row(segment, my_row, my_layer, n_layer):
    first, second, _, other = segment
    layer = (n_layer - 1 - my_layer) if other else my_layer
    return my_row ^ jnp.where(layer == 0, first, second)


def panel_kernel(sizes, segments, where_ref, *refs):
    n_row, n_col, n_layer, listed, side = sizes
    arrays = len(segments)
    array_refs = refs[:arrays]
    panel, table, buffer, lists, sem = refs[arrays:]
    nblk = ROW_BLOCKS * n_row
    cblk = nblk // n_col
    half = ROW_BLOCKS // n_layer
    my_col, my_layer = where_ref[1], where_ref[2]
    moves = start_copies(side, listed, array_refs, buffer, lists, sem)
    nxt, tag = nblk, nblk + arrays * listed
    total = tag + arrays * listed

    def clear(i, _):
        table[i] = -1
        return 0

    lax.fori_loop(0, nblk, clear, 0)
    count = jnp.int32(0)
    for i, (value, names) in enumerate(moves):
        names.wait()
        value.wait()
        first = lax.rem(my_col + (n_col - segments[i][2]), n_col) * cblk

        def one(s, count, i=i, first=first):
            code = lists[i, s].astype(jnp.int32)
            key = first + (code & 15)
            mark = (code >> 4) - my_layer * half
            use = (code >= 0) & (mark >= 0) & (mark < half)

            @pl.when(use)
            def _():
                table[nxt + count] = table[key]
                table[key] = count
                table[tag + count] = mark
                high, low = split(buffer[lanes(i * listed + s, side), :])
                panel[count, :, :side] = high
                panel[count, :, side:] = low

            return count + use.astype(jnp.int32)

        count = lax.fori_loop(0, listed, one, count)
    table[total] = count
    for i in range(3):
        table[total + 1 + i] = where_ref[i]


def panel_call(sizes, segments, arrays, where):
    n_row, n_col, n_layer, listed, side = sizes
    nblk = ROW_BLOCKS * n_row
    total = len(segments) * listed
    return pl.pallas_call(
        functools.partial(panel_kernel, sizes, segments),
        out_shape=[
            jax.ShapeDtypeStruct((total, side, 2 * side), jnp.bfloat16),
            jax.ShapeDtypeStruct((nblk + 2 * total + 4,), jnp.int32),
        ],
        in_specs=[SMEM] + [HBM] * len(arrays),
        out_specs=[VMEM, SMEM],
        scratch_shapes=[
            pltpu.VMEM((total * side, side), jnp.float32),
            pltpu.SMEM((len(segments), side), jnp.float32),
            pltpu.SemaphoreType.DMA((2, len(segments))),
        ],
        compiler_params=params(max(PANEL_MB, total // 4)),
        name="left_panel",
    )(where, *arrays)


def tile_kernel(sizes, shifts, segments, *refs):
    n_row, n_col, n_layer, listed, side = sizes
    arrays = len(segments)
    table, left_ref = refs[:2]
    array_refs = refs[2 : 2 + arrays]
    rest = refs[2 + arrays :]
    if shifts[0]:
        column_refs, before, rest = rest[: n_layer * 4], rest[n_layer * 4], rest[n_layer * 4 + 1 :]
    else:
        column_refs = array_refs
    (out_hbm, buffer, lists, sem, left, left_sem, column, column_lists, column_sem) = rest[:9]
    late, out_sem, out_ref, right, panel, square, wide, plan, cubes = rest[9:]
    nblk = ROW_BLOCKS * n_row
    cblk = nblk // n_col
    rows = ROW_BLOCKS // n_layer * side
    pairs = n_layer * listed
    nxt, tag = nblk, nblk + left.shape[0]
    total = tag + left.shape[0]
    my_row, my_col, my_layer = table[total + 1], table[total + 2], table[total + 3]
    moves = start_copies(side, listed, array_refs, buffer, lists, sem)

    def get_left(i):
        part = pl.ds(pl.multiple_of(i * listed, listed), listed)
        return pltpu.make_async_copy(left_ref.at[part], left.at[part], left_sem.at[i])

    def each_left(step):
        def one(i, _):
            step(get_left(i))
            return 0

        lax.fori_loop(0, (table[total] + listed - 1) // listed, one, 0)

    each_left(lambda copy: copy.start())

    cols = [lax.rem(my_col + (n_col - shift), n_col) for shift in shifts]
    meets = [col * cblk // ROW_BLOCKS for col in cols]

    def get_column(t, ref, copy):
        at = (t * n_layer + copy) * listed * side
        return (
            pltpu.make_async_copy(
                ref.at[pl.ds(0, listed * side)],
                column.at[pl.ds(at, listed * side)],
                column_sem.at[0, t * n_layer + copy],
            ),
            pltpu.make_async_copy(
                ref.at[pl.ds(listed * side, 1)],
                column_lists.at[pl.ds(t * n_layer + copy, 1)],
                column_sem.at[1, t * n_layer + copy],
            ),
        )

    for t in range(len(shifts)):
        for i in range(n_layer * 4):
            first, second, _, other = segments[i % 4]
            copy = i // 4
            layer = (n_layer - 1 - my_layer) if copy else my_layer

            @pl.when((my_row ^ jnp.where(layer == 0, first, second)) == meets[t])
            def _(t=t, i=i, copy=copy):
                for move in get_column(t, column_refs[i], copy):
                    move.start()

    def put(i):
        line = pl.ds(pl.multiple_of(i * STRIP, STRIP), STRIP)
        return pltpu.make_async_copy(out_ref.at[line], out_hbm.at[line], out_sem.at[i])

    if shifts[0]:
        get_before = pltpu.make_async_copy(before, out_ref, late)
        get_before.start()

    for t, shift in enumerate(shifts):

        def zero(j, _):
            square[j] = jnp.zeros((rows, side), jnp.float32)
            return 0

        lax.fori_loop(0, cblk, zero, 0)
        count = jnp.int32(0)
        for i, (value, names) in enumerate(moves):
            if segments[i][2] != shift:
                continue
            names.wait()
            value.wait()
            row0 = tile_row(segments[i], my_row, my_layer, n_layer) * ROW_BLOCKS

            def one(s, count, i=i, row0=row0):
                code = lists[i, s].astype(jnp.int32)
                local = code & 15
                first = jnp.where(code >= 0, table[jnp.maximum(row0 + (code >> 4), 0)], -1)
                at = i * listed + s

                @pl.when(first >= 0)
                def _():
                    high, low = split(buffer[lanes(at, side), :])
                    right[at, :, :side] = high
                    right[at, :, side:] = low

                def more(carry):
                    return carry[0] >= 0

                def add(carry):
                    a, count = carry
                    plan[0, count] = a
                    plan[1, count] = at
                    plan[2, count] = local
                    plan[3, count] = table[tag + a]
                    return table[nxt + a], count + 1

                return lax.while_loop(more, add, (first, count))[1]

            count = lax.fori_loop(0, listed, one, count)

        for u in range(GROUP - 1):
            plan[0, count + u] = 0
            plan[1, count + u] = 0
            plan[2, count + u] = cblk
            plan[3, count + u] = 0

        def group(g, _):
            parts = []
            for u in range(GROUP):
                e = g * GROUP + u
                parts.append(product(left[plan[0, e]], right[plan[1, e]]))
            for u in range(GROUP):
                e = g * GROUP + u
                at = lanes(plan[3, e], side)
                j = plan[2, e]
                square[j, at, :] = square[j, at, :] + parts[u]
            return 0

        if not t:
            each_left(lambda copy: copy.wait())
        lax.fori_loop(0, (count + GROUP - 1) // GROUP, group, 0)
        if not shift:

            def begin(j, _):
                out_ref[:, lanes(j, side)] = 3.0 * square[j]
                return 0

            lax.fori_loop(0, cblk, begin, 0)
        elif not t:
            get_before.wait()

        def widen(j, _):
            high, low = split(-2.0 * square[j])
            wide[j, :, :side] = high
            wide[j, :, side:] = low
            return 0

        lax.fori_loop(0, cblk, widen, 0)
        for copy in range(n_layer):
            for move in get_column(t, column_refs[0], copy):
                move.wait()
        start = meets[t] * ROW_BLOCKS - cols[t] * cblk

        def note(e, count, t=t, start=start):
            copy = e // listed
            code = column_lists[t * n_layer + copy, e - copy * listed].astype(jnp.int32)
            j = start + (code >> 4)
            use = (code >= 0) & (j >= 0) & (j < cblk)

            @pl.when(use)
            def _():
                high, low = split(column[lanes(t * pairs + e, side), :])
                panel[e, :, :side] = high
                panel[e, :, side:] = low
                cubes[0, count] = e
                cubes[1, count] = j
                cubes[2, count] = code & 15

            return count + use.astype(jnp.int32)

        count = lax.fori_loop(0, pairs, note, jnp.int32(0))
        wide[cblk] = jnp.zeros((rows, 2 * side), jnp.bfloat16)
        for u in range(CUBES - 1):
            cubes[0, count + u] = cubes[0, 0]
            cubes[1, count + u] = cblk
            cubes[2, count + u] = 0

        final = t == len(shifts) - 1

        def strip(i, _, count=count, final=final):
            def cube(g, _):
                for m in range(0, STRIP, CHUNK):
                    line = pl.ds(pl.multiple_of(i * STRIP + m, CHUNK), CHUNK)
                    parts = []
                    for u in range(CUBES):
                        e = g * CUBES + u
                        parts.append(product(wide[cubes[1, e], line, :], panel[cubes[0, e]]))
                    for u in range(CUBES):
                        at = lanes(cubes[2, g * CUBES + u], side)
                        out_ref[line, at] = out_ref[line, at] + parts[u]
                return 0

            lax.fori_loop(0, (count + CUBES - 1) // CUBES, cube, 0)
            if final:
                put(i).start()
            return 0

        lax.fori_loop(0, rows // STRIP, strip, 0)

    def written(i, _):
        put(i).wait()
        return 0

    lax.fori_loop(0, rows // STRIP, written, 0)


def tile_call(sizes, shifts, segments, arrays, lefts, column, before):
    n_row, n_col, n_layer, listed, side = sizes
    nblk = ROW_BLOCKS * n_row
    cblk = nblk // n_col
    half = ROW_BLOCKS // n_layer
    rows = half * side
    total = len(segments) * listed
    pairs = n_layer * listed
    left, table = lefts
    extra = [] if before is None else [*column, before]
    return pl.pallas_call(
        functools.partial(tile_kernel, sizes, shifts, segments),
        out_shape=jax.ShapeDtypeStruct((rows, cblk * side), jnp.float32),
        in_specs=[SMEM] + [HBM] * (1 + len(arrays) + len(extra)),
        out_specs=HBM,
        scratch_shapes=[
            pltpu.VMEM((total * side, side), jnp.float32),
            pltpu.SMEM((len(segments), side), jnp.float32),
            pltpu.SemaphoreType.DMA((2, len(segments))),
            pltpu.VMEM(left.shape, left.dtype),
            pltpu.SemaphoreType.DMA((left.shape[0] // listed,)),
            pltpu.VMEM((len(shifts) * pairs * side, side), jnp.float32),
            pltpu.SMEM((len(shifts) * n_layer, side), jnp.float32),
            pltpu.SemaphoreType.DMA((2, len(shifts) * n_layer)),
            pltpu.SemaphoreType.DMA,
            pltpu.SemaphoreType.DMA((rows // STRIP,)),
            pltpu.VMEM((rows, cblk * side), jnp.float32),
            pltpu.VMEM((total, side, 2 * side), jnp.bfloat16),
            pltpu.VMEM((pairs, side, 2 * side), jnp.bfloat16),
            pltpu.VMEM((cblk + 1, rows, side), jnp.float32),
            pltpu.VMEM((cblk + 1, rows, 2 * side), jnp.bfloat16),
            pltpu.SMEM((4, total * half + GROUP), jnp.int32),
            pltpu.SMEM((3, pairs + CUBES), jnp.int32),
        ],
        compiler_params=params(TILE_MB),
        name="tiles_" + "_".join(str(s) for s in shifts),
    )(table, left, *arrays, *extra)


def shards(blocks, block_ids, counts):
    n_row, n_col, n_layer = (lax.axis_size(a) for a in AXES)
    listed, side = blocks.shape[3], blocks.shape[-1]
    sizes = (n_row, n_col, n_layer, listed, side)
    half = ROW_BLOCKS // n_layer

    def flip(bits, cross=False):
        pairs = []
        for r in range(n_row):
            for k in range(n_layer):
                to = n_layer - 1 - k if cross else k
                pairs.append((r * n_layer + k, (r ^ bits[min(k, 1)]) * n_layer + to))
        return lambda y: lax.ppermute(y, ("row", "layer"), pairs)

    across, along, beside = flip((1, 2)), flip((2, 1)), flip((2, 1), True)

    def ring(y):
        return lax.ppermute(y, "col", [(i, (i + 1) % n_col) for i in range(n_col)])

    def sibling(y):
        return lax.ppermute(y, "layer", [(i, n_layer - 1 - i) for i in range(n_layer)])

    where = jnp.stack([lax.axis_index(a) for a in AXES]).astype(jnp.int32)
    cblk = ROW_BLOCKS * n_row // n_col
    ids = block_ids.reshape(1, listed)
    live = lax.broadcasted_iota(jnp.int32, (1, listed), 1) < counts.reshape(1, 1)
    names = jnp.where(live, ids // cblk * 16 + ids % cblk, -1).astype(jnp.float32)
    names = jnp.pad(names, ((0, 7), (0, side - listed)))
    own = jnp.concatenate([blocks.reshape(listed * side, side), names], axis=0)

    ways = {"A": (0, 0), "U": (1, 2), "V": (2, 1), "D": (3, 3)}
    held = {("A", 0): own}
    twin = {}
    lefts = total = None
    fresh = [("A", 0)]

    def gathered(names):
        segments = [(*ways[k], s, other) for other in (False, True) for k, s in names]
        return segments, [source[name] for source in (held, twin) for name in names]

    def quads(shifts):
        return [(k, s) for s in shifts for k in ways]

    def tiles(shifts, total):
        for i in range(0, len(shifts), 2):
            segments, arrays = gathered(quads(shifts[i : i + 2]))
            column = gathered(quads([0]))[1]
            total = tile_call(
                sizes, tuple(shifts[i : i + 2]), segments, arrays, lefts, column, total
            )
        return total

    rounds = [[] for _ in range(2 * n_col)]
    for s in range(n_col):
        if s:
            rounds[s - 1].append((("A", s), s - 1))
        first = AHEAD[min(s, 3)] + max(0, s - 3)
        there = first + LATER[min(s, 3)]
        rounds[first] += [(("U", s), there), (("V", s), there)]
        rounds[there + 1].append((("D", s), there + 1))
    last = max(t for t in range(2 * n_col) if rounds[t])
    makers = {
        "A": lambda s: ring(held[("A", s - 1)]),
        "U": lambda s: across(held[("A", s)]),
        "V": lambda s: along(held[("A", s)]),
        "D": lambda s: along(held[("U", s)]),
    }
    done = 0
    flying = {}
    for t in range(last + 2):
        for name, there in rounds[t]:
            flying[name] = (makers[name[0]](name[1]), there)
            if t == last:
                twin[name] = beside(held[("U", name[1])])
        twin.update({name: sibling(held[name]) for name in fresh if name not in twin})
        if lefts is None and ("A", n_col - 1) in twin:
            segments, arrays = gathered([("A", s) for s in range(n_col)])
            lefts = panel_call(sizes, segments, arrays, where)
        ready = done
        while lefts is not None and ready < n_col and {("D", ready)} <= held.keys() & twin.keys():
            ready += 1
        total = tiles(list(range(done, ready)), total)
        done = ready
        if t > last:
            return total
        sent = {n: flying.pop(n)[0] for n in list(flying) if flying[n][1] == t}
        copied = {n: twin[n] for n in [*fresh, *sent] if n in twin}
        sent, copied, lefts, total = lax.optimization_barrier((sent, copied, lefts, total))
        held.update(sent)
        twin.update(copied)
        fresh = list(sent)


def solution(mesh):
    return jax.shard_map(
        shards,
        mesh=mesh,
        in_specs=(
            P("row", "col", "layer", None, None, None),
            P("row", "col", "layer", None),
            P("row", "col", "layer"),
        ),
        out_specs=P(("row", "layer"), "col"),
        check_vma=False,
    )
```

```python
import functools

import jax
import jax.numpy as jnp
from jax import lax
from jax.experimental import pallas as pl
from jax.experimental.pallas import tpu as pltpu
from jax.sharding import PartitionSpec as P

ROW_BLOCKS = 12
GROUP = 4
CUBES = 8
CHUNK = 128
STRIP = 384
TILE_MB = 61
AXES = ("row", "col", "layer")
VMEM = pl.BlockSpec(memory_space=pltpu.VMEM)
SMEM = pl.BlockSpec(memory_space=pltpu.SMEM)
HBM = pl.BlockSpec(memory_space=pltpu.HBM)


def params(megabytes):
    return pltpu.CompilerParams(vmem_limit_bytes=megabytes * 1024 * 1024)


def split(x):
    high = x.astype(jnp.bfloat16)
    low = (x - high.astype(jnp.float32)).astype(jnp.bfloat16)
    return high, low


def product(left, right):
    part = jnp.dot(
        left, jnp.concatenate([right, right], axis=0), preferred_element_type=jnp.float32
    )
    side = right.shape[0]
    return part[:, :side] + part[:, side:]


def lanes(i, side):
    return pl.ds(pl.multiple_of(i * side, side), side)


def start_copies(side, listed, array_refs, buffer, lists, sem):
    out = []
    for i, ref in enumerate(array_refs):
        value = pltpu.make_async_copy(
            ref.at[pl.ds(0, listed * side)],
            buffer.at[pl.ds(i * listed * side, listed * side)],
            sem.at[0, i],
        )
        names = pltpu.make_async_copy(
            ref.at[pl.ds(listed * side, 1)], lists.at[pl.ds(i, 1)], sem.at[1, i]
        )
        value.start()
        names.start()
        out.append((value, names))
    return out


def tile_row(segment, my_row, my_layer, n_layer):
    first, second, _, other = segment
    layer = (n_layer - 1 - my_layer) if other else my_layer
    return my_row ^ jnp.where(layer == 0, first, second)


def build_left(sizes, segments, where_ref, moves, buffer, lists, left, table):
    n_row, n_col, n_layer, listed, side = sizes
    nblk = ROW_BLOCKS * n_row
    cblk = nblk // n_col
    half = ROW_BLOCKS // n_layer
    my_col, my_layer = where_ref[1], where_ref[2]
    nxt, tag = nblk, nblk + left.shape[0]
    total = tag + left.shape[0]

    def clear(i, _):
        table[i] = -1
        return 0

    lax.fori_loop(0, nblk, clear, 0)
    count = jnp.int32(0)
    for i, (value, names) in enumerate(moves):
        names.wait()
        value.wait()
        first = lax.rem(my_col + (n_col - segments[i][2]), n_col) * cblk

        def one(s, count, i=i, first=first):
            code = lists[i, s].astype(jnp.int32)
            key = first + (code & 15)
            mark = (code >> 4) - my_layer * half
            use = (code >= 0) & (mark >= 0) & (mark < half)

            @pl.when(use)
            def _():
                table[nxt + count] = table[key]
                table[key] = count
                table[tag + count] = mark
                high, low = split(buffer[lanes(i * listed + s, side), :])
                left[count, :, :side] = high
                left[count, :, side:] = low

            return count + use.astype(jnp.int32)

        count = lax.fori_loop(0, listed, one, count)
    table[total] = count
    for i in range(3):
        table[total + 1 + i] = where_ref[i]


def tile_kernel(sizes, shifts, segments, builds, *refs):
    n_row, n_col, n_layer, listed, side = sizes
    arrays = len(segments)
    if builds:
        where_ref, array_refs = refs[0], refs[1 : 1 + arrays]
        build_refs = refs[1 + arrays : 1 + arrays + len(builds)]
        rest = refs[1 + arrays + len(builds) :]
    else:
        table, left_ref = refs[:2]
        array_refs = refs[2 : 2 + arrays]
        rest = refs[2 + arrays :]
    if shifts[0]:
        column_refs, before, rest = rest[: n_layer * 4], rest[n_layer * 4], rest[n_layer * 4 + 1 :]
    else:
        column_refs = array_refs
    if builds:
        out_hbm, left_ref, table, *rest, build_buffer, build_lists, build_sem = rest
    else:
        out_hbm, *rest = rest
    (buffer, lists, sem, left, left_sem, column, column_lists, column_sem) = rest[:8]
    late, out_sem, out_ref, right, panel, square, wide, plan, cubes = rest[8:]
    nblk = ROW_BLOCKS * n_row
    cblk = nblk // n_col
    rows = ROW_BLOCKS // n_layer * side
    pairs = n_layer * listed
    nxt, tag = nblk, nblk + left.shape[0]
    total = tag + left.shape[0]
    if builds:
        my_row, my_col, my_layer = where_ref[0], where_ref[1], where_ref[2]
        built = start_copies(side, listed, build_refs, build_buffer, build_lists, build_sem)
    else:
        my_row, my_col, my_layer = table[total + 1], table[total + 2], table[total + 3]
    moves = start_copies(side, listed, array_refs, buffer, lists, sem)

    def get_left(i):
        part = pl.ds(pl.multiple_of(i * listed, listed), listed)
        if builds:
            return pltpu.make_async_copy(left.at[part], left_ref.at[part], left_sem.at[i])
        return pltpu.make_async_copy(left_ref.at[part], left.at[part], left_sem.at[i])

    def each_left(step):
        def one(i, _):
            step(get_left(i))
            return 0

        lax.fori_loop(0, (table[total] + listed - 1) // listed, one, 0)

    if not builds:
        each_left(lambda copy: copy.start())

    cols = [lax.rem(my_col + (n_col - shift), n_col) for shift in shifts]
    meets = [col * cblk // ROW_BLOCKS for col in cols]

    def get_column(t, ref, copy):
        at = (t * n_layer + copy) * listed * side
        return (
            pltpu.make_async_copy(
                ref.at[pl.ds(0, listed * side)],
                column.at[pl.ds(at, listed * side)],
                column_sem.at[0, t * n_layer + copy],
            ),
            pltpu.make_async_copy(
                ref.at[pl.ds(listed * side, 1)],
                column_lists.at[pl.ds(t * n_layer + copy, 1)],
                column_sem.at[1, t * n_layer + copy],
            ),
        )

    for t in range(len(shifts)):
        for i in range(n_layer * 4):
            first, second, _, other = segments[i % 4]
            copy = i // 4
            layer = (n_layer - 1 - my_layer) if copy else my_layer

            @pl.when((my_row ^ jnp.where(layer == 0, first, second)) == meets[t])
            def _(t=t, i=i, copy=copy):
                for move in get_column(t, column_refs[i], copy):
                    move.start()

    def put(i):
        line = pl.ds(pl.multiple_of(i * STRIP, STRIP), STRIP)
        return pltpu.make_async_copy(out_ref.at[line], out_hbm.at[line], out_sem.at[i])

    if shifts[0]:
        get_before = pltpu.make_async_copy(before, out_ref, late)
        get_before.start()

    if builds:
        build_left(sizes, builds, where_ref, built, build_buffer, build_lists, left, table)
        each_left(lambda copy: copy.start())

    for t, shift in enumerate(shifts):

        def zero(j, _):
            square[j] = jnp.zeros((rows, side), jnp.float32)
            return 0

        lax.fori_loop(0, cblk, zero, 0)
        count = jnp.int32(0)
        for i, (value, names) in enumerate(moves):
            if segments[i][2] != shift:
                continue
            names.wait()
            value.wait()
            row0 = tile_row(segments[i], my_row, my_layer, n_layer) * ROW_BLOCKS

            def one(s, count, i=i, row0=row0):
                code = lists[i, s].astype(jnp.int32)
                local = code & 15
                first = jnp.where(code >= 0, table[jnp.maximum(row0 + (code >> 4), 0)], -1)
                at = i * listed + s

                @pl.when(first >= 0)
                def _():
                    high, low = split(buffer[lanes(at, side), :])
                    right[at, :, :side] = high
                    right[at, :, side:] = low

                def more(carry):
                    return carry[0] >= 0

                def add(carry):
                    a, count = carry
                    plan[0, count] = a
                    plan[1, count] = at
                    plan[2, count] = local
                    plan[3, count] = table[tag + a]
                    return table[nxt + a], count + 1

                return lax.while_loop(more, add, (first, count))[1]

            count = lax.fori_loop(0, listed, one, count)

        for u in range(GROUP - 1):
            plan[0, count + u] = 0
            plan[1, count + u] = 0
            plan[2, count + u] = cblk
            plan[3, count + u] = 0

        def group(g, _):
            parts = []
            for u in range(GROUP):
                e = g * GROUP + u
                parts.append(product(left[plan[0, e]], right[plan[1, e]]))
            for u in range(GROUP):
                e = g * GROUP + u
                at = lanes(plan[3, e], side)
                j = plan[2, e]
                square[j, at, :] = square[j, at, :] + parts[u]
            return 0

        if not t and not builds:
            each_left(lambda copy: copy.wait())
        lax.fori_loop(0, (count + GROUP - 1) // GROUP, group, 0)
        if not shift:

            def begin(j, _):
                out_ref[:, lanes(j, side)] = 3.0 * square[j]
                return 0

            lax.fori_loop(0, cblk, begin, 0)
        elif not t:
            get_before.wait()

        def widen(j, _):
            high, low = split(-2.0 * square[j])
            wide[j, :, :side] = high
            wide[j, :, side:] = low
            return 0

        lax.fori_loop(0, cblk, widen, 0)
        for copy in range(n_layer):
            for move in get_column(t, column_refs[0], copy):
                move.wait()
        start = meets[t] * ROW_BLOCKS - cols[t] * cblk

        def note(e, count, t=t, start=start):
            copy = e // listed
            code = column_lists[t * n_layer + copy, e - copy * listed].astype(jnp.int32)
            j = start + (code >> 4)
            use = (code >= 0) & (j >= 0) & (j < cblk)

            @pl.when(use)
            def _():
                high, low = split(column[lanes(t * pairs + e, side), :])
                panel[e, :, :side] = high
                panel[e, :, side:] = low
                cubes[0, count] = e
                cubes[1, count] = j
                cubes[2, count] = code & 15

            return count + use.astype(jnp.int32)

        count = lax.fori_loop(0, pairs, note, jnp.int32(0))
        wide[cblk] = jnp.zeros((rows, 2 * side), jnp.bfloat16)
        for u in range(CUBES - 1):
            cubes[0, count + u] = cubes[0, 0]
            cubes[1, count + u] = cblk
            cubes[2, count + u] = 0

        final = t == len(shifts) - 1

        def strip(i, _, count=count, final=final):
            def cube(g, _):
                for m in range(0, STRIP, CHUNK):
                    line = pl.ds(pl.multiple_of(i * STRIP + m, CHUNK), CHUNK)
                    parts = []
                    for u in range(CUBES):
                        e = g * CUBES + u
                        parts.append(product(wide[cubes[1, e], line, :], panel[cubes[0, e]]))
                    for u in range(CUBES):
                        at = lanes(cubes[2, g * CUBES + u], side)
                        out_ref[line, at] = out_ref[line, at] + parts[u]
                return 0

            lax.fori_loop(0, (count + CUBES - 1) // CUBES, cube, 0)
            if final:
                put(i).start()
            return 0

        lax.fori_loop(0, rows // STRIP, strip, 0)

    def written(i, _):
        put(i).wait()
        return 0

    lax.fori_loop(0, rows // STRIP, written, 0)
    if builds:
        each_left(lambda copy: copy.wait())


def tile_call(sizes, shifts, segments, arrays, builds, built, where, lefts, column, before):
    n_row, n_col, n_layer, listed, side = sizes
    nblk = ROW_BLOCKS * n_row
    cblk = nblk // n_col
    half = ROW_BLOCKS // n_layer
    rows = half * side
    total = len(segments) * listed
    pairs = n_layer * listed
    lines = n_col * n_layer * listed
    out = jax.ShapeDtypeStruct((rows, cblk * side), jnp.float32)
    left = jax.ShapeDtypeStruct((lines, side, 2 * side), jnp.bfloat16)
    table = jax.ShapeDtypeStruct((nblk + 2 * lines + 4,), jnp.int32)
    extra = [] if before is None else [*column, before]
    scratch = [
        pltpu.VMEM((total * side, side), jnp.float32),
        pltpu.SMEM((len(segments), side), jnp.float32),
        pltpu.SemaphoreType.DMA((2, len(segments))),
        pltpu.VMEM(left.shape, left.dtype),
        pltpu.SemaphoreType.DMA((lines // listed,)),
        pltpu.VMEM((len(shifts) * pairs * side, side), jnp.float32),
        pltpu.SMEM((len(shifts) * n_layer, side), jnp.float32),
        pltpu.SemaphoreType.DMA((2, len(shifts) * n_layer)),
        pltpu.SemaphoreType.DMA,
        pltpu.SemaphoreType.DMA((rows // STRIP,)),
        pltpu.VMEM((rows, cblk * side), jnp.float32),
        pltpu.VMEM((total, side, 2 * side), jnp.bfloat16),
        pltpu.VMEM((pairs, side, 2 * side), jnp.bfloat16),
        pltpu.VMEM((cblk + 1, rows, side), jnp.float32),
        pltpu.VMEM((cblk + 1, rows, 2 * side), jnp.bfloat16),
        pltpu.SMEM((4, total * half + GROUP), jnp.int32),
        pltpu.SMEM((3, pairs + CUBES), jnp.int32),
    ]
    if builds:
        scratch += [
            pltpu.VMEM((lines * side, side), jnp.float32),
            pltpu.SMEM((len(builds), side), jnp.float32),
            pltpu.SemaphoreType.DMA((2, len(builds))),
        ]
    call = pl.pallas_call(
        functools.partial(tile_kernel, sizes, shifts, segments, builds),
        out_shape=[out, left, table] if builds else out,
        in_specs=[SMEM] + [HBM] * (len(arrays) + len(extra) + (len(built) if builds else 1)),
        out_specs=[HBM, HBM, SMEM] if builds else HBM,
        scratch_shapes=scratch,
        compiler_params=params(TILE_MB),
        name="tiles_" + "_".join(str(s) for s in shifts),
    )
    if builds:
        out, left, table = call(where, *arrays, *built)
        return out, (left, table)
    left, table = lefts
    return call(table, left, *arrays, *extra), lefts


def shards(blocks, block_ids, counts):
    n_row, n_col, n_layer = (lax.axis_size(a) for a in AXES)
    listed, side = blocks.shape[3], blocks.shape[-1]
    sizes = (n_row, n_col, n_layer, listed, side)
    half = ROW_BLOCKS // n_layer

    def flip(bits, cross=False):
        pairs = []
        for r in range(n_row):
            for k in range(n_layer):
                to = n_layer - 1 - k if cross else k
                pairs.append((r * n_layer + k, (r ^ bits[min(k, 1)]) * n_layer + to))
        return lambda y: lax.ppermute(y, ("row", "layer"), pairs)

    across, along, beside = flip((1, 2)), flip((2, 1)), flip((2, 1), True)

    def ring(y):
        return lax.ppermute(y, "col", [(i, (i + 1) % n_col) for i in range(n_col)])

    def sibling(y):
        return lax.ppermute(y, "layer", [(i, n_layer - 1 - i) for i in range(n_layer)])

    where = jnp.stack([lax.axis_index(a) for a in AXES]).astype(jnp.int32)
    cblk = ROW_BLOCKS * n_row // n_col
    ids = block_ids.reshape(1, listed)
    live = lax.broadcasted_iota(jnp.int32, (1, listed), 1) < counts.reshape(1, 1)
    names = jnp.where(live, ids // cblk * 16 + ids % cblk, -1).astype(jnp.float32)
    names = jnp.pad(names, ((0, 7), (0, side - listed)))
    own = jnp.concatenate([blocks.reshape(listed * side, side), names], axis=0)

    ways = {"A": (0, 0), "U": (1, 2), "V": (2, 1), "D": (3, 3)}
    held = {("A", 0): own}
    twin = {}
    lefts = total = None
    fresh = [("A", 0)]

    def gathered(names):
        segments = [(*ways[k], s, other) for other in (False, True) for k, s in names]
        return segments, [source[name] for source in (held, twin) for name in names]

    def quads(shifts):
        return [(k, s) for s in shifts for k in ways]

    def tiles(shifts, total, lefts):
        for i in range(0, len(shifts), 2):
            segments, arrays = gathered(quads(shifts[i : i + 2]))
            builds, built = [], []
            if lefts is None:
                builds, built = gathered([("A", s) for s in range(n_col)])
            column = gathered(quads([0]))[1]
            total, lefts = tile_call(
                sizes,
                tuple(shifts[i : i + 2]),
                segments,
                arrays,
                builds,
                built,
                where,
                lefts,
                column,
                total,
            )
        return total, lefts

    rounds = [[] for _ in range(n_col + 3)]
    for s in range(n_col):
        if s:
            rounds[s - 1].append(("A", s))
        rounds[s].append(("U", s))
        rounds[s + min(s, 1)].append(("V", s))
        rounds[s + min(s, 1) + 1].append(("D", s))
    last = max(t for t in range(n_col + 3) if rounds[t])
    makers = {
        "A": lambda s: ring(held[("A", s - 1)]),
        "U": lambda s: across(held[("A", s)]),
        "V": lambda s: along(held[("A", s)]),
        "D": lambda s: along(held[("U", s)]),
    }
    done = 0
    for t in range(last + 2):
        sent = {}
        for name in rounds[t] if t <= last else []:
            sent[name] = makers[name[0]](name[1])
            if t == last:
                twin[name] = beside(held[("U", name[1])])
        twin.update({name: sibling(held[name]) for name in fresh if name not in twin})
        ready = done
        while ("A", n_col - 1) in twin and ready < n_col and {("D", ready)} <= held.keys() & twin.keys():
            ready += 1
        total, lefts = tiles(list(range(done, ready)), total, lefts)
        done = ready
        if t > last:
            return total
        copied = {n: twin[n] for n in [*fresh, *sent] if n in twin}
        sent, copied, lefts, total = lax.optimization_barrier((sent, copied, lefts, total))
        held.update(sent)
        twin.update(copied)
        fresh = list(sent)


def solution(mesh):
    return jax.shard_map(
        shards,
        mesh=mesh,
        in_specs=(
            P("row", "col", "layer", None, None, None),
            P("row", "col", "layer", None),
            P("row", "col", "layer"),
        ),
        out_specs=P(("row", "layer"), "col"),
        check_vma=False,
    )
```

```python
import functools

import jax
import jax.numpy as jnp
from jax import lax
from jax.experimental import pallas as pl
from jax.experimental.pallas import tpu as pltpu
from jax.sharding import PartitionSpec as P

ROW_BLOCKS = 12
GROUP = 8
CUBES = 8
CHUNK = 128
STRIP = 384
TILE_MB = 61
AXES = ("row", "col", "layer")
VMEM = pl.BlockSpec(memory_space=pltpu.VMEM)
SMEM = pl.BlockSpec(memory_space=pltpu.SMEM)
HBM = pl.BlockSpec(memory_space=pltpu.HBM)


def params(megabytes):
    return pltpu.CompilerParams(vmem_limit_bytes=megabytes * 1024 * 1024)


def split(x):
    high = x.astype(jnp.bfloat16)
    low = (x - high.astype(jnp.float32)).astype(jnp.bfloat16)
    return high, low


def product(left, right):
    part = jnp.dot(
        left, jnp.concatenate([right, right], axis=0), preferred_element_type=jnp.float32
    )
    side = right.shape[0]
    return part[:, :side] + part[:, side:]


def lanes(i, side):
    return pl.ds(pl.multiple_of(i * side, side), side)


def start_copies(side, listed, array_refs, buffer, lists, sem):
    out = []
    for i, ref in enumerate(array_refs):
        value = pltpu.make_async_copy(
            ref.at[pl.ds(0, listed * side)],
            buffer.at[pl.ds(i * listed * side, listed * side)],
            sem.at[0, i],
        )
        names = pltpu.make_async_copy(
            ref.at[pl.ds(listed * side, 1)], lists.at[pl.ds(i, 1)], sem.at[1, i]
        )
        value.start()
        names.start()
        out.append((value, names))
    return out


def tile_row(segment, my_row, my_layer, n_layer):
    first, second, _, other = segment
    layer = (n_layer - 1 - my_layer) if other else my_layer
    return my_row ^ jnp.where(layer == 0, first, second)


def build_left(sizes, segments, where_ref, moves, buffer, lists, left, table):
    n_row, n_col, n_layer, listed, side = sizes
    nblk = ROW_BLOCKS * n_row
    cblk = nblk // n_col
    half = ROW_BLOCKS // n_layer
    my_col, my_layer = where_ref[1], where_ref[2]
    nxt, tag = nblk, nblk + left.shape[0]
    total = tag + left.shape[0]

    def clear(i, _):
        table[i] = -1
        return 0

    lax.fori_loop(0, nblk, clear, 0)
    count = jnp.int32(0)
    for i, (value, names) in enumerate(moves):
        names.wait()
        value.wait()
        first = lax.rem(my_col + (n_col - segments[i][2]), n_col) * cblk

        def one(s, count, i=i, first=first):
            code = lists[i, s].astype(jnp.int32)
            key = first + (code & 15)
            mark = (code >> 4) - my_layer * half
            use = (code >= 0) & (mark >= 0) & (mark < half)

            @pl.when(use)
            def _():
                table[nxt + count] = table[key]
                table[key] = count
                table[tag + count] = mark
                high, low = split(buffer[lanes(i * listed + s, side), :])
                left[count, :, :side] = high
                left[count, :, side:] = low

            return count + use.astype(jnp.int32)

        count = lax.fori_loop(0, listed, one, count)
    table[total] = count
    for i in range(3):
        table[total + 1 + i] = where_ref[i]


def tile_kernel(sizes, shifts, segments, builds, *refs):
    n_row, n_col, n_layer, listed, side = sizes
    arrays = len(segments)
    if builds:
        where_ref, array_refs = refs[0], refs[1 : 1 + arrays]
        build_refs = refs[1 + arrays : 1 + arrays + len(builds)]
        rest = refs[1 + arrays + len(builds) :]
    else:
        table, left_ref = refs[:2]
        array_refs = refs[2 : 2 + arrays]
        rest = refs[2 + arrays :]
    if shifts[0]:
        column_refs, before, rest = rest[: n_layer * 4], rest[n_layer * 4], rest[n_layer * 4 + 1 :]
    else:
        column_refs = array_refs
    if builds:
        out_hbm, left_ref, table, *rest, build_buffer, build_lists, build_sem = rest
    else:
        out_hbm, *rest = rest
    (buffer, lists, sem, left, left_sem, column, column_lists, column_sem) = rest[:8]
    late, out_sem, out_ref, right, panel, square, wide, plan, cubes = rest[8:]
    nblk = ROW_BLOCKS * n_row
    cblk = nblk // n_col
    rows = ROW_BLOCKS // n_layer * side
    pairs = n_layer * listed
    nxt, tag = nblk, nblk + left.shape[0]
    total = tag + left.shape[0]
    if builds:
        my_row, my_col, my_layer = where_ref[0], where_ref[1], where_ref[2]
        built = start_copies(side, listed, build_refs, build_buffer, build_lists, build_sem)
    else:
        my_row, my_col, my_layer = table[total + 1], table[total + 2], table[total + 3]
    moves = start_copies(side, listed, array_refs, buffer, lists, sem)

    def get_left(i):
        part = pl.ds(pl.multiple_of(i * listed, listed), listed)
        if builds:
            return pltpu.make_async_copy(left.at[part], left_ref.at[part], left_sem.at[i])
        return pltpu.make_async_copy(left_ref.at[part], left.at[part], left_sem.at[i])

    def each_left(step):
        def one(i, _):
            step(get_left(i))
            return 0

        lax.fori_loop(0, (table[total] + listed - 1) // listed, one, 0)

    if not builds:
        each_left(lambda copy: copy.start())

    cols = [lax.rem(my_col + (n_col - shift), n_col) for shift in shifts]
    meets = [col * cblk // ROW_BLOCKS for col in cols]

    def get_column(t, ref, copy):
        at = (t * n_layer + copy) * listed * side
        return (
            pltpu.make_async_copy(
                ref.at[pl.ds(0, listed * side)],
                column.at[pl.ds(at, listed * side)],
                column_sem.at[0, t * n_layer + copy],
            ),
            pltpu.make_async_copy(
                ref.at[pl.ds(listed * side, 1)],
                column_lists.at[pl.ds(t * n_layer + copy, 1)],
                column_sem.at[1, t * n_layer + copy],
            ),
        )

    for t in range(len(shifts)):
        for i in range(n_layer * 4):
            first, second, _, other = segments[i % 4]
            copy = i // 4
            layer = (n_layer - 1 - my_layer) if copy else my_layer

            @pl.when((my_row ^ jnp.where(layer == 0, first, second)) == meets[t])
            def _(t=t, i=i, copy=copy):
                for move in get_column(t, column_refs[i], copy):
                    move.start()

    def put(i):
        line = pl.ds(pl.multiple_of(i * STRIP, STRIP), STRIP)
        return pltpu.make_async_copy(out_ref.at[line], out_hbm.at[line], out_sem.at[i])

    if shifts[0]:
        get_before = pltpu.make_async_copy(before, out_ref, late)
        get_before.start()

    if builds:
        build_left(sizes, builds, where_ref, built, build_buffer, build_lists, left, table)
        each_left(lambda copy: copy.start())

    for t, shift in enumerate(shifts):

        def zero(j, _):
            square[j] = jnp.zeros((rows, side), jnp.float32)
            return 0

        lax.fori_loop(0, cblk, zero, 0)
        count = jnp.int32(0)
        for i, (value, names) in enumerate(moves):
            if segments[i][2] != shift:
                continue
            names.wait()
            value.wait()
            row0 = tile_row(segments[i], my_row, my_layer, n_layer) * ROW_BLOCKS

            def one(s, count, i=i, row0=row0):
                code = lists[i, s].astype(jnp.int32)
                local = code & 15
                first = jnp.where(code >= 0, table[jnp.maximum(row0 + (code >> 4), 0)], -1)
                at = i * listed + s

                @pl.when(first >= 0)
                def _():
                    high, low = split(buffer[lanes(at, side), :])
                    right[at, :, :side] = high
                    right[at, :, side:] = low

                def more(carry):
                    return carry[0] >= 0

                def add(carry):
                    a, count = carry
                    plan[0, count] = a
                    plan[1, count] = at
                    plan[2, count] = local
                    plan[3, count] = table[tag + a]
                    return table[nxt + a], count + 1

                return lax.while_loop(more, add, (first, count))[1]

            count = lax.fori_loop(0, listed, one, count)

        for u in range(GROUP - 1):
            plan[0, count + u] = 0
            plan[1, count + u] = 0
            plan[2, count + u] = cblk
            plan[3, count + u] = 0

        def group(g, _):
            parts = []
            for u in range(GROUP):
                e = g * GROUP + u
                parts.append(product(left[plan[0, e]], right[plan[1, e]]))
            for u in range(GROUP):
                e = g * GROUP + u
                at = lanes(plan[3, e], side)
                j = plan[2, e]
                square[j, at, :] = square[j, at, :] + parts[u]
            return 0

        if not t and not builds:
            each_left(lambda copy: copy.wait())
        lax.fori_loop(0, (count + GROUP - 1) // GROUP, group, 0)
        if not shift:

            def begin(j, _):
                out_ref[:, lanes(j, side)] = 3.0 * square[j]
                return 0

            lax.fori_loop(0, cblk, begin, 0)
        elif not t:
            get_before.wait()

        def widen(j, _):
            high, low = split(-2.0 * square[j])
            wide[j, :, :side] = high
            wide[j, :, side:] = low
            return 0

        lax.fori_loop(0, cblk, widen, 0)
        for copy in range(n_layer):
            for move in get_column(t, column_refs[0], copy):
                move.wait()
        start = meets[t] * ROW_BLOCKS - cols[t] * cblk

        def note(e, count, t=t, start=start):
            copy = e // listed
            code = column_lists[t * n_layer + copy, e - copy * listed].astype(jnp.int32)
            j = start + (code >> 4)
            use = (code >= 0) & (j >= 0) & (j < cblk)

            @pl.when(use)
            def _():
                high, low = split(column[lanes(t * pairs + e, side), :])
                panel[e, :, :side] = high
                panel[e, :, side:] = low
                cubes[0, count] = e
                cubes[1, count] = j
                cubes[2, count] = code & 15

            return count + use.astype(jnp.int32)

        count = lax.fori_loop(0, pairs, note, jnp.int32(0))
        wide[cblk] = jnp.zeros((rows, 2 * side), jnp.bfloat16)
        for u in range(CUBES - 1):
            cubes[0, count + u] = cubes[0, 0]
            cubes[1, count + u] = cblk
            cubes[2, count + u] = 0

        final = t == len(shifts) - 1

        def strip(i, _, count=count, final=final):
            def cube(g, _):
                for m in range(0, STRIP, CHUNK):
                    line = pl.ds(pl.multiple_of(i * STRIP + m, CHUNK), CHUNK)
                    parts = []
                    for u in range(CUBES):
                        e = g * CUBES + u
                        parts.append(product(wide[cubes[1, e], line, :], panel[cubes[0, e]]))
                    for u in range(CUBES):
                        at = lanes(cubes[2, g * CUBES + u], side)
                        out_ref[line, at] = out_ref[line, at] + parts[u]
                return 0

            lax.fori_loop(0, (count + CUBES - 1) // CUBES, cube, 0)
            if final:
                put(i).start()
            return 0

        lax.fori_loop(0, rows // STRIP, strip, 0)

    def written(i, _):
        put(i).wait()
        return 0

    lax.fori_loop(0, rows // STRIP, written, 0)
    if builds:
        each_left(lambda copy: copy.wait())


def tile_call(sizes, shifts, segments, arrays, builds, built, where, lefts, column, before):
    n_row, n_col, n_layer, listed, side = sizes
    nblk = ROW_BLOCKS * n_row
    cblk = nblk // n_col
    half = ROW_BLOCKS // n_layer
    rows = half * side
    total = len(segments) * listed
    pairs = n_layer * listed
    lines = n_col * n_layer * listed
    out = jax.ShapeDtypeStruct((rows, cblk * side), jnp.float32)
    left = jax.ShapeDtypeStruct((lines, side, 2 * side), jnp.bfloat16)
    table = jax.ShapeDtypeStruct((nblk + 2 * lines + 4,), jnp.int32)
    extra = [] if before is None else [*column, before]
    scratch = [
        pltpu.VMEM((total * side, side), jnp.float32),
        pltpu.SMEM((len(segments), side), jnp.float32),
        pltpu.SemaphoreType.DMA((2, len(segments))),
        pltpu.VMEM(left.shape, left.dtype),
        pltpu.SemaphoreType.DMA((lines // listed,)),
        pltpu.VMEM((len(shifts) * pairs * side, side), jnp.float32),
        pltpu.SMEM((len(shifts) * n_layer, side), jnp.float32),
        pltpu.SemaphoreType.DMA((2, len(shifts) * n_layer)),
        pltpu.SemaphoreType.DMA,
        pltpu.SemaphoreType.DMA((rows // STRIP,)),
        pltpu.VMEM((rows, cblk * side), jnp.float32),
        pltpu.VMEM((total, side, 2 * side), jnp.bfloat16),
        pltpu.VMEM((pairs, side, 2 * side), jnp.bfloat16),
        pltpu.VMEM((cblk + 1, rows, side), jnp.float32),
        pltpu.VMEM((cblk + 1, rows, 2 * side), jnp.bfloat16),
        pltpu.SMEM((4, total * half + GROUP), jnp.int32),
        pltpu.SMEM((3, pairs + CUBES), jnp.int32),
    ]
    if builds:
        scratch += [
            pltpu.VMEM((lines * side, side), jnp.float32),
            pltpu.SMEM((len(builds), side), jnp.float32),
            pltpu.SemaphoreType.DMA((2, len(builds))),
        ]
    call = pl.pallas_call(
        functools.partial(tile_kernel, sizes, shifts, segments, builds),
        out_shape=[out, left, table] if builds else out,
        in_specs=[SMEM] + [HBM] * (len(arrays) + len(extra) + (len(built) if builds else 1)),
        out_specs=[HBM, HBM, SMEM] if builds else HBM,
        scratch_shapes=scratch,
        compiler_params=params(TILE_MB),
        name="tiles_" + "_".join(str(s) for s in shifts),
    )
    if builds:
        out, left, table = call(where, *arrays, *built)
        return out, (left, table)
    left, table = lefts
    return call(table, left, *arrays, *extra), lefts


def shards(blocks, block_ids, counts):
    n_row, n_col, n_layer = (lax.axis_size(a) for a in AXES)
    listed, side = blocks.shape[3], blocks.shape[-1]
    sizes = (n_row, n_col, n_layer, listed, side)
    half = ROW_BLOCKS // n_layer

    def flip(bits, cross=False):
        pairs = []
        for r in range(n_row):
            for k in range(n_layer):
                to = n_layer - 1 - k if cross else k
                pairs.append((r * n_layer + k, (r ^ bits[min(k, 1)]) * n_layer + to))
        return lambda y: lax.ppermute(y, ("row", "layer"), pairs)

    across, along, beside = flip((1, 2)), flip((2, 1)), flip((2, 1), True)

    def ring(y):
        return lax.ppermute(y, "col", [(i, (i + 1) % n_col) for i in range(n_col)])

    def sibling(y):
        return lax.ppermute(y, "layer", [(i, n_layer - 1 - i) for i in range(n_layer)])

    where = jnp.stack([lax.axis_index(a) for a in AXES]).astype(jnp.int32)
    cblk = ROW_BLOCKS * n_row // n_col
    ids = block_ids.reshape(1, listed)
    live = lax.broadcasted_iota(jnp.int32, (1, listed), 1) < counts.reshape(1, 1)
    names = jnp.where(live, ids // cblk * 16 + ids % cblk, -1).astype(jnp.float32)
    names = jnp.pad(names, ((0, 7), (0, side - listed)))
    own = jnp.concatenate([blocks.reshape(listed * side, side), names], axis=0)

    ways = {"A": (0, 0), "U": (1, 2), "V": (2, 1), "D": (3, 3)}
    held = {("A", 0): own}
    twin = {}
    lefts = total = None
    fresh = [("A", 0)]

    def gathered(names):
        segments = [(*ways[k], s, other) for other in (False, True) for k, s in names]
        return segments, [source[name] for source in (held, twin) for name in names]

    def quads(shifts):
        return [(k, s) for s in shifts for k in ways]

    def tiles(shifts, total, lefts):
        for i in range(0, len(shifts), 2):
            segments, arrays = gathered(quads(shifts[i : i + 2]))
            builds, built = [], []
            if lefts is None:
                builds, built = gathered([("A", s) for s in range(n_col)])
            column = gathered(quads([0]))[1]
            total, lefts = tile_call(
                sizes,
                tuple(shifts[i : i + 2]),
                segments,
                arrays,
                builds,
                built,
                where,
                lefts,
                column,
                total,
            )
        return total, lefts

    rounds = [[] for _ in range(n_col + 3)]
    for s in range(n_col):
        if s:
            rounds[s - 1].append(("A", s))
        rounds[s].append(("U", s))
        rounds[s + min(s, 1)].append(("V", s))
        rounds[s + min(s, 1) + 1].append(("D", s))
    last = max(t for t in range(n_col + 3) if rounds[t])
    makers = {
        "A": lambda s: ring(held[("A", s - 1)]),
        "U": lambda s: across(held[("A", s)]),
        "V": lambda s: along(held[("A", s)]),
        "D": lambda s: along(held[("U", s)]),
    }
    done = 0
    for t in range(last + 2):
        sent = {}
        for name in rounds[t] if t <= last else []:
            sent[name] = makers[name[0]](name[1])
            if t == last:
                twin[name] = beside(held[("U", name[1])])
        twin.update({name: sibling(held[name]) for name in fresh if name not in twin})
        ready = done
        while ("A", n_col - 1) in twin and ready < n_col and {("D", ready)} <= held.keys() & twin.keys():
            ready += 1
        total, lefts = tiles(list(range(done, ready)), total, lefts)
        done = ready
        if t > last:
            return total
        copied = {n: twin[n] for n in [*fresh, *sent] if n in twin}
        sent, copied, lefts, total = lax.optimization_barrier((sent, copied, lefts, total))
        held.update(sent)
        twin.update(copied)
        fresh = list(sent)


def solution(mesh):
    return jax.shard_map(
        shards,
        mesh=mesh,
        in_specs=(
            P("row", "col", "layer", None, None, None),
            P("row", "col", "layer", None),
            P("row", "col", "layer"),
        ),
        out_specs=P(("row", "layer"), "col"),
        check_vma=False,
    )
```
